32 devices in a mesh: dp: 4 (over y, core), fsdp: 8 (over z, x).
Axes of the slice: x: 2, y: 2, z: 4, core: 2. Of those that a mesh axis runs over, the one named last changes fastest.
Arguments:
- tokens: bfloat16 [32768, 768], P(('dp', 'fsdp')), may hold values from -6 to 6
- cotangent: bfloat16 [32768, 768], P(('dp', 'fsdp')), may hold values from -6 to 6
- segment_ids: int32 [64, 512], P(('dp', 'fsdp')), may hold values from 0 to 47, never falling along the last dimension, each value on 1 to 16 neighbouring positions
- w_attn: float32 [768, 2304], P('fsdp'), may hold values from -0.3125 to 0.3125
- moment_attn: float32 [768, 2304], P('fsdp'), may hold values from -543.058 to 543.058
- square_attn: float32 [768, 2304], P('fsdp'), may hold values from 3276.8 to 26214.4
- w_proj: float32 [768, 768], P('fsdp'), may hold values from -0.4375 to 0.4375
- moment_proj: float32 [768, 768], P('fsdp'), may hold values from -543.058 to 543.058
- square_proj: float32 [768, 768], P('fsdp'), may hold values from 3276.8 to 26214.4
- w_up: float32 [768, 3072], P('fsdp'), may hold values from -0.21875 to 0.21875
- moment_up: float32 [768, 3072], P('fsdp'), may hold values from -543.058 to 543.058
- square_up: float32 [768, 3072], P('fsdp'), may hold values from 3276.8 to 26214.4
- w_down: float32 [3072, 768], P('fsdp'), may hold values from -0.15625 to 0.15625
- moment_down: float32 [3072, 768], P('fsdp'), may hold values from -543.058 to 543.058
- square_down: float32 [3072, 768], P('fsdp'), may hold values from 3276.8 to 26214.4
- vectors: float32 [768, 12], P('fsdp'), may hold values from -1.2 to 1.3
- moment_vec: float32 [768, 12], P('fsdp'), may hold values from -905.0967 to 905.0967
- square_vec: float32 [768, 12], P('fsdp'), may hold values from 16384 to 131072
Outputs:
- block_out: bfloat16 [32768, 768], P(('dp', 'fsdp'))
- grad_tokens: float32 [32768, 768], P(('dp', 'fsdp'))
- attn_new: float32 [768, 2304], P('fsdp')
- attn_moment: float32 [768, 2304], P('fsdp')
- attn_square: float32 [768, 2304], P('fsdp')
- proj_new: float32 [768, 768], P('fsdp')
- proj_moment: float32 [768, 768], P('fsdp')
- proj_square: float32 [768, 768], P('fsdp')
- up_new: float32 [768, 3072], P('fsdp')
- up_moment: float32 [768, 3072], P('fsdp')
- up_square: float32 [768, 3072], P('fsdp')
- down_new: float32 [3072, 768], P('fsdp')
- down_moment: float32 [3072, 768], P('fsdp')
- down_square: float32 [3072, 768], P('fsdp')
- vec_new: float32 [768, 12], P('fsdp')
- vec_moment: float32 [768, 12], P('fsdp')
- vec_square: float32 [768, 12], P('fsdp')
The draws below stay inside these ranges and needn't reach their ends.
Inputs may be any that keep to these rules, and one draw needn't show every extreme that they name: `segment_ids`: ids never fall along a block; each caption holds 1 to 16 rows, one of them exactly 16.
All inputs are finite; a program needn't handle non-finite values.
Results may differ from the reference program's by a relative error of at most 0.012.
The reference program's roundings to bfloat16 on the way count: a program that leaves them out, or rounds other values in their place, can miss the bound.
Values may be sent and summed in bfloat16 or wider, within the bound.
No kernel may reach another device: no remote copies, remote signals or barrier semaphores. Data moves between devices by JAX's collectives and lax.ppermute only.
A program may use at most 192 MiB of HBM per device.

```python
import math
import jax
import jax.numpy as jnp
import numpy as np
from jax import lax

D = 768
HEADS = 12
HEAD = 64
FF = 3072
PACK = 512
MOST = 16
COUNT = 48
STEP = 5
PACKS = 64
TOKENS = 32768


def draw_vectors(key, part):
    first, second = jax.random.split(key)
    column = jnp.arange(12, dtype=jnp.int32)[None, :] + jnp.zeros((D, 12), jnp.int32)
    shifts = 0.3 * jax.random.truncated_normal(first, -4.0, 4.0, (D, 12), jnp.float32)
    gains = 1.0 + 0.3 * jax.random.uniform(second, (D, 12), jnp.float32, -1.0, 1.0)
    is_gain = (column == 0) | (column == 5)
    return jnp.where(is_gain, gains, shifts)


def level_of(rng, shape, pieces, low, largest):
    def one(axis_at, parts):
        draws = jax.random.uniform(jax.random.fold_in(jax.random.fold_in(rng, 6), axis_at), (parts,), jnp.float32, low / len(pieces), largest / len(pieces))
        return jnp.repeat(jnp.exp(draws), shape[axis_at] // parts).reshape((-1,) + (1,) * (len(shape) - axis_at - 1))

    gain = one(*pieces[0])
    for cut in pieces[1:]:
        gain = gain * one(*cut)
    return gain


def profile(number_of, total, bound, lean):
    loads = [(1 << 20) // math.isqrt(grade ** lean) + 1 for grade in range(2, number_of + 1)]
    rest, holding = total - bound - (number_of - 1), [1] * (number_of - 1)
    while rest > 0:
        candidates = [i for i in range(number_of - 1) if holding[i] < bound]
        whole, budget = sum([loads[i] for i in candidates]), rest
        for i in candidates:
            extra = min(bound - holding[i], max(1, budget * loads[i] // whole), rest)
            holding[i] = holding[i] + extra
            rest = rest - extra
    return np.array([bound] + holding)


def ragged_sizes(own_key, number_of, total, limit, lean):
    if number_of == 2:
        one = jax.random.randint(own_key, (), max(1, total - limit), min(limit, total - 1) + 1)
        return jnp.stack([one, total - one])
    tallies = jnp.asarray(profile(number_of, total, limit, lean), jnp.int32)
    couples = (number_of - 1) // 2
    donor, receiver = tallies[1:1 + 2 * couples:2], tallies[2:2 + 2 * couples:2]
    margin = jnp.minimum(donor - 1, limit - receiver)
    shifted = jax.random.randint(jax.random.fold_in(own_key, 1), (couples,), 0, 1 << 20) % (margin + 1)
    tallies = tallies.at[1:1 + 2 * couples:2].set(donor - shifted).at[2:2 + 2 * couples:2].set(receiver + shifted)
    return tallies[jax.random.permutation(jax.random.fold_in(own_key, 2), number_of)]


def bell_draw(stream_key, dims, spread, reach, shards=(), held_as=jnp.bfloat16):
    drawn = jax.random.normal(stream_key, dims, jnp.float32) * spread
    if len(shards) > 0:
        drawn = level_of(stream_key, dims, shards, -0.22, 0.18) * drawn
    return jnp.clip(drawn, min=-reach, max=reach).astype(held_as)


def setup_inputs(seed: int = 0) -> dict:
    streams_of = jax.random.split(jax.random.key(seed), 19)
    tokens = bell_draw(streams_of[0], (TOKENS, D), 1.0, 6.0, ((0, 32),))
    cotangent = bell_draw(streams_of[1], (TOKENS, D), 1.0, 6.0, ((0, 32),))
    segment_ids = jax.vmap(lambda own: jnp.searchsorted(jnp.cumsum(ragged_sizes(own, COUNT, PACK, MOST, 1)), jnp.arange(PACK), side="right"))(jax.random.split(streams_of[2], PACKS)).reshape((PACKS, PACK)).astype(jnp.int32)
    w_attn = bell_draw(streams_of[3], (D, 3 * D), (D // 2) ** -0.5, 0.3125, ((0, 8),), jnp.float32)
    moment_attn = bell_draw(streams_of[4], (D, 3 * D), (0.5 * TOKENS ** 0.5), 543.058, ((0, 8),), jnp.float32)
    square_attn = jnp.clip(jnp.exp(math.log(26214.4) - 2.0794415 * jax.random.uniform(streams_of[5], (D, 3 * D), jnp.float32) ** level_of(streams_of[5], (D, 3 * D), ((0, 8),), -0.2, 0.2)), 3276.8, 26214.4)
    w_proj = bell_draw(streams_of[6], (D, D), (D // 4) ** -0.5, 0.4375, ((0, 8),), jnp.float32)
    moment_proj = bell_draw(streams_of[7], (D, D), (0.5 * TOKENS ** 0.5), 543.058, ((0, 8),), jnp.float32)
    square_proj = jnp.clip(jnp.exp(math.log(26214.4) - 2.0794415 * jax.random.uniform(streams_of[8], (D, D), jnp.float32) ** level_of(streams_of[8], (D, D), ((0, 8),), -0.2, 0.2)), 3276.8, 26214.4)
    w_up = bell_draw(streams_of[9], (D, FF), D ** -0.5, 0.21875, ((0, 8),), jnp.float32)
    moment_up = bell_draw(streams_of[10], (D, FF), (0.5 * TOKENS ** 0.5), 543.058, ((0, 8),), jnp.float32)
    square_up = jnp.clip(jnp.exp(math.log(26214.4) - 2.0794415 * jax.random.uniform(streams_of[11], (D, FF), jnp.float32) ** level_of(streams_of[11], (D, FF), ((0, 8),), -0.2, 0.2)), 3276.8, 26214.4)
    w_down = bell_draw(streams_of[12], (FF, D), (FF // 2) ** -0.5, 0.15625, ((0, 8),), jnp.float32)
    moment_down = bell_draw(streams_of[13], (FF, D), (0.5 * TOKENS ** 0.5), 543.058, ((0, 8),), jnp.float32)
    square_down = jnp.clip(jnp.exp(math.log(26214.4) - 2.0794415 * jax.random.uniform(streams_of[14], (FF, D), jnp.float32) ** level_of(streams_of[14], (FF, D), ((0, 8),), -0.2, 0.2)), 3276.8, 26214.4)
    vectors = draw_vectors(jax.random.fold_in(streams_of[18], 71), 0)
    moment_vec = bell_draw(streams_of[16], (D, 12), (TOKENS ** 0.5), 905.0967, ((0, 8),), jnp.float32)
    square_vec = jnp.clip(jnp.exp(math.log(131072.0) - 2.0794415 * jax.random.uniform(streams_of[17], (D, 12), jnp.float32) ** level_of(streams_of[17], (D, 12), ((0, 8),), -0.2, 0.2)), 16384.0, 131072.0)
    return dict(tokens=tokens, cotangent=cotangent, segment_ids=segment_ids, w_attn=w_attn, moment_attn=moment_attn, square_attn=square_attn, w_proj=w_proj, moment_proj=moment_proj, square_proj=square_proj, w_up=w_up, moment_up=moment_up, square_up=square_up, w_down=w_down, moment_down=moment_down, square_down=square_down, vectors=vectors, moment_vec=moment_vec, square_vec=square_vec)


@jax.custom_vjp
def low(v):
    return lax.optimization_barrier(v.astype(jnp.bfloat16)).astype(jnp.float32)

@jax.custom_vjp
def low_back(v):
    return v

def low_keep(v):
    return (low(v), None)

def low_pass(kept, grad):
    return (grad,)

def back_keep(v):
    return (v, None)

def back_low(kept, grad):
    return (low(grad),)
low.defvjp(low_keep, low_pass)
low_back.defvjp(back_keep, back_low)
eps_norm = 1e-06
beta_one = 0.5
beta_two = 0.5
rate_matrix = 0.03
rate_vector = 0.25
weight_decay = 0.1
eps_adam = 1e-08
masked_score = -1e+30
group_packs = 8

def layer_norm(rows_in, gain_vec, shift_vec):
    row_mean = lax.optimization_barrier(jnp.mean(rows_in, axis=-1, keepdims=True))
    centered = rows_in - row_mean
    row_var = lax.optimization_barrier(jnp.mean(centered * centered, axis=-1, keepdims=True))
    return centered * lax.rsqrt(row_var + eps_norm) * gain_vec + shift_vec

def unpack_vectors(packed_vec):
    return (packed_vec[:, 0], packed_vec[:, 1], packed_vec[:, 2], packed_vec[:, 3], packed_vec[:, 4], packed_vec[:, 5], packed_vec[:, 6], packed_vec[:, 7], packed_vec[:, 8:12].T.reshape(FF))

def attend_pack(packed):
    qkv_pack, seg_pack = packed
    queries = qkv_pack[:, :D].reshape(PACK, HEADS, HEAD)
    key_rows = qkv_pack[:, D:2 * D].reshape(PACK, HEADS, HEAD)
    values = qkv_pack[:, 2 * D:].reshape(PACK, HEADS, HEAD)
    scores = jnp.einsum('qhd,khd->hqk', queries, key_rows, precision=lax.Precision.HIGHEST) * HEAD ** (-0.5)
    scores = low_back(scores)
    same_caption = seg_pack[:, None] == seg_pack[None, :]
    scores = jnp.where(same_caption[None], scores, masked_score)
    soft_weights = low(jax.nn.softmax(scores, axis=-1))
    mixed_pack = jnp.einsum('hqk,khd->qhd', soft_weights, values, precision=lax.Precision.HIGHEST)
    return mixed_pack.reshape(PACK, D)

def forward(inputs, w_attn, w_proj, w_up, w_down, vectors, segments):
    w_attn = low(w_attn)
    w_proj = low(w_proj)
    w_up = low(w_up)
    w_down = low(w_down)
    gain_one, shift_one, q_bias, v_bias, out_bias, gain_two, shift_two, down_bias, up_bias = unpack_vectors(low(vectors))
    normed_one = low(layer_norm(inputs, gain_one, shift_one))
    qkv_bias = jnp.concatenate([q_bias, jnp.zeros_like(q_bias), v_bias])
    qkv = low_back(low(jnp.dot(normed_one, w_attn, precision=lax.Precision.HIGHEST) + qkv_bias))
    pack_count = inputs.shape[0] // PACK
    mixed_rows = lax.map(jax.checkpoint(attend_pack), (qkv.reshape(pack_count, PACK, 3 * D), segments))
    mixed_rows = low_back(low(mixed_rows.reshape(pack_count * PACK, D)))
    branch = low_back(jnp.dot(mixed_rows, w_proj, precision=lax.Precision.HIGHEST) + out_bias)
    residual = inputs + branch
    normed_two = low(layer_norm(residual, gain_two, shift_two))
    pre_act = low_back(jnp.dot(normed_two, w_up, precision=lax.Precision.HIGHEST) + up_bias)
    activated = low(jax.nn.gelu(pre_act))
    mlp_out = low_back(jnp.dot(activated, w_down, precision=lax.Precision.HIGHEST) + down_bias)
    return residual + mlp_out

def adam_step(master, moment, square, gradient, rate, decay_rate):
    moment_new = beta_one * moment + (1.0 - beta_one) * gradient
    square_new = beta_two * square + (1.0 - beta_two) * gradient * gradient
    moment_hat = moment_new / (1.0 - beta_one ** STEP)
    square_hat = square_new / (1.0 - beta_two ** STEP)
    master_new = master - rate * (moment_hat / (jnp.sqrt(square_hat) + eps_adam) + decay_rate * master)
    return (master_new, moment_new, square_new)

def reference(tokens, cotangent, segment_ids, w_attn, moment_attn, square_attn, w_proj, moment_proj, square_proj, w_up, moment_up, square_up, w_down, moment_down, square_down, vectors, moment_vec, square_vec):
    group_rows = group_packs * PACK
    group_count = tokens.shape[0] // group_rows
    blocks = (tokens.astype(jnp.float32).reshape(group_count, group_rows, D), cotangent.astype(jnp.float32).reshape(group_count, group_rows, D), segment_ids.reshape(group_count, group_packs, PACK))
    weights = (w_attn, w_proj, w_up, w_down, vectors)

    def group_step(running, block):
        inputs_rows, grad_rows, seg_rows = block

        def run(inputs_in, attn_in, proj_in, up_in, down_in, vec_in):
            return forward(inputs_in, attn_in, proj_in, up_in, down_in, vec_in, seg_rows)
        outputs, pull = jax.vjp(run, inputs_rows, w_attn, w_proj, w_up, w_down, vectors)
        grads_all = pull(grad_rows)
        running = tuple((total_in + grad_term for total_in, grad_term in zip(running, grads_all[1:])))
        return (running, (outputs.astype(jnp.bfloat16), grads_all[0]))
    zeros_init = tuple((jnp.zeros(weight_in.shape, jnp.float32) for weight_in in weights))
    totals, (out_rows, grad_rows_all) = lax.scan(group_step, zeros_init, blocks)
    attn_upd = adam_step(w_attn, moment_attn, square_attn, totals[0], rate_matrix, weight_decay)
    proj_upd = adam_step(w_proj, moment_proj, square_proj, totals[1], rate_matrix, weight_decay)
    up_upd = adam_step(w_up, moment_up, square_up, totals[2], rate_matrix, weight_decay)
    down_upd = adam_step(w_down, moment_down, square_down, totals[3], rate_matrix, weight_decay)
    vec_upd = adam_step(vectors, moment_vec, square_vec, totals[4], rate_vector, 0.0)
    return (out_rows.reshape(tokens.shape[0], D), grad_rows_all.reshape(tokens.shape[0], D), attn_upd[0], attn_upd[1], attn_upd[2], proj_upd[0], proj_upd[1], proj_upd[2], up_upd[0], up_upd[1], up_upd[2], down_upd[0], down_upd[1], down_upd[2], vec_upd[0], vec_upd[1], vec_upd[2])
```

```python
import functools

import jax
import jax.numpy as jnp
from jax import lax
from jax.sharding import PartitionSpec as P

D = 768
HEADS = 12
HEAD = 64
FF = 3072
PACK = 512
STEP = 5


eps_norm = 1e-06
beta_one = 0.5
beta_two = 0.5
rate_matrix = 0.03
rate_vector = 0.25
weight_decay = 0.1
eps_adam = 1e-08
masked_score = -1e30


def layer_norm(rows_in, gain_vec, shift_vec):
    row_mean = jnp.mean(rows_in, axis=-1, keepdims=True)
    centered = rows_in - row_mean
    row_var = jnp.mean(centered * centered, axis=-1, keepdims=True)
    return centered * lax.rsqrt(row_var + eps_norm) * gain_vec + shift_vec


def contract_rows(left, right):
    return lax.dot_general(
        left, right, (((0,), (0,)), ((), ())), preferred_element_type=jnp.float32
    )


def contract_cols(left, right):
    return lax.dot_general(
        left, right, (((1,), (1,)), ((), ())), preferred_element_type=jnp.float32
    )


def scores_of(qkv_pack, seg_pack):
    queries = qkv_pack[:, :D].reshape(PACK, HEADS, HEAD)
    key_rows = qkv_pack[:, D : 2 * D].reshape(PACK, HEADS, HEAD)
    values = qkv_pack[:, 2 * D :].reshape(PACK, HEADS, HEAD)
    scores = jnp.einsum(
        "qhd,khd->hqk", queries, key_rows, preferred_element_type=jnp.float32
    ) * HEAD ** (-0.5)
    same_caption = seg_pack[:, None] == seg_pack[None, :]
    scores = jnp.where(same_caption[None], scores, masked_score)
    return (queries, key_rows, values, scores)


def attend(packed):
    qkv_pack, seg_pack = packed
    queries, key_rows, values, scores = scores_of(qkv_pack, seg_pack)
    row_max = jnp.max(scores, axis=-1, keepdims=True)
    exp_scores = jnp.exp(scores - row_max)
    exp_total = jnp.sum(exp_scores, axis=-1, keepdims=True)
    soft_weights = (exp_scores / exp_total).astype(jnp.bfloat16)
    mixed_pack = jnp.einsum(
        "hqk,khd->qhd", soft_weights, values, preferred_element_type=jnp.float32
    )
    return (
        mixed_pack.reshape(PACK, D).astype(jnp.bfloat16),
        (row_max + jnp.log(exp_total))[..., 0],
    )


def attend_back(packed):
    qkv_pack, seg_pack, log_total, grad_pack = packed
    queries, key_rows, values, scores = scores_of(qkv_pack, seg_pack)
    soft_exact = jnp.exp(scores - log_total[..., None])
    grad_heads = grad_pack.reshape(PACK, HEADS, HEAD)
    grad_soft = jnp.einsum("qhd,khd->hqk", grad_heads, values, preferred_element_type=jnp.float32)
    row_delta = jnp.sum(soft_exact * grad_soft, axis=-1, keepdims=True)
    grad_score = (soft_exact * (grad_soft - row_delta)).astype(jnp.bfloat16)
    score_scale = HEAD ** (-0.5)
    grad_queries = (
        jnp.einsum("hqk,khd->qhd", grad_score, key_rows, preferred_element_type=jnp.float32)
        * score_scale
    )
    grad_keys = (
        jnp.einsum("hqk,qhd->khd", grad_score, queries, preferred_element_type=jnp.float32)
        * score_scale
    )
    grad_values = jnp.einsum(
        "hqk,qhd->khd",
        soft_exact.astype(jnp.bfloat16),
        grad_heads,
        preferred_element_type=jnp.float32,
    )
    joined = jnp.concatenate(
        [grad_queries.reshape(PACK, D), grad_keys.reshape(PACK, D), grad_values.reshape(PACK, D)],
        axis=1,
    )
    return joined.astype(jnp.bfloat16)


ALL_AXES = ("dp", "fsdp")


def take(array, index, axis):
    return lax.dynamic_index_in_dim(array, index, axis, keepdims=False)


def make_comm(mesh):
    dp_size, fsdp_size = mesh.shape["dp"], mesh.shape["fsdp"]

    def gather_rows(shard):
        rows, cols = shard.shape
        piece = rows // dp_size
        mine = lax.dynamic_slice_in_dim(shard, lax.axis_index("dp") * piece, piece, 0)
        full = lax.all_gather(mine, ALL_AXES, axis=0, tiled=True)
        full = full.reshape(dp_size, fsdp_size, piece, cols)
        return full.transpose(1, 0, 2, 3).reshape(fsdp_size * rows, cols)

    def reduce_plain(grad, first):
        part = lax.psum_scatter(grad, "fsdp", scatter_dimension=0, tiled=True)
        return lax.psum(part, "dp")

    def place(dev):
        return dev // 16, dev // 8 % 2, dev // 2 % 4, dev % 2

    def index(y, c, z, x):
        return y * 16 + c * 8 + z * 2 + x

    def swap(array, move):
        pairs = [(dev, index(*move(*place(dev)))) for dev in range(32)]
        return lax.ppermute(array, ALL_AXES, pairs)

    def swap_c(array):
        return swap(array, lambda y, c, z, x: (y, 1 - c, z, x))

    def swap_y(array):
        return swap(array, lambda y, c, z, x: (1 - y, c, z, x))

    def swap_x(array):
        return swap(array, lambda y, c, z, x: (y, c, z, 1 - x))

    def turn_z(array, step):
        return swap(array, lambda y, c, z, x: (y, c, (z + step) % 4, x))

    def reduce_tree(grad, first):
        dp_at, fsdp_at = lax.axis_index("dp"), lax.axis_index("fsdp")
        y_at, c_at, z_at, x_at = dp_at // 2, dp_at % 2, fsdp_at // 2, fsdp_at % 2
        rows, cols = grad.shape[0] // 32, grad.shape[1]
        low = grad.astype(jnp.bfloat16).reshape(4, 2, 2, 2, rows, cols)

        def add(kept, came):
            return (kept.astype(jnp.float32) + came.astype(jnp.float32)).astype(jnp.bfloat16)

        part = add(take(low, c_at, 3), swap_c(take(low, 1 - c_at, 3)))
        if first == "y":
            part = add(take(part, y_at, 2), swap_y(take(part, 1 - y_at, 2)))
            part = add(take(part, x_at, 1), swap_x(take(part, 1 - x_at, 1)))
        else:
            part = add(take(part, x_at, 1), swap_x(take(part, 1 - x_at, 1)))
            part = add(take(part, y_at, 1), swap_y(take(part, 1 - y_at, 1)))
        total = take(part, z_at, 0).astype(jnp.float32)
        for step in (2, 1, 3):
            total += turn_z(take(part, (z_at + step) % 4, 0), step).astype(jnp.float32)
        total = total.astype(jnp.bfloat16)
        other = swap_y(total)
        pair = jnp.stack(
            [jnp.where(y_at == 0, total, other), jnp.where(y_at == 0, other, total)]
        )
        other = swap_c(pair)
        quad = jnp.stack(
            [jnp.where(c_at == 0, pair, other), jnp.where(c_at == 0, other, pair)], axis=1
        )
        return quad.reshape(4 * rows, cols).astype(jnp.float32)

    tree = dp_size == 4 and fsdp_size == 8
    return gather_rows, reduce_tree if tree else reduce_plain


def adam_step(master, moment, square, gradient, rate, decay_rate):
    moment_new = beta_one * moment + (1.0 - beta_one) * gradient
    square_new = beta_two * square + (1.0 - beta_two) * gradient * gradient
    moment_hat = moment_new / (1.0 - beta_one**STEP)
    square_hat = square_new / (1.0 - beta_two**STEP)
    master_new = master - rate * (
        moment_hat / (jnp.sqrt(square_hat) + eps_adam) + decay_rate * master
    )
    return (master_new, moment_new, square_new)


def body(
    gather_rows,
    reduce_rows,
    tokens,
    cotangent,
    segment_ids,
    w_attn,
    moment_attn,
    square_attn,
    w_proj,
    moment_proj,
    square_proj,
    w_up,
    moment_up,
    square_up,
    w_down,
    moment_down,
    square_down,
    vectors,
    moment_vec,
    square_vec,
):
    low_attn = w_attn.astype(jnp.bfloat16)
    low_proj = w_proj.astype(jnp.bfloat16)
    low_up = w_up.astype(jnp.bfloat16)
    low_down = w_down.astype(jnp.bfloat16)
    low_vec = vectors.astype(jnp.bfloat16)
    first_block = jnp.concatenate(
        [low_attn, jnp.pad(low_vec, ((0, 0), (0, 128 - low_vec.shape[1])))], axis=1
    )
    full_first = gather_rows(first_block)
    full_attn, full_vec = full_first[:, : 3 * D], full_first[:, 3 * D : 3 * D + 12]
    full_proj, full_up, full_down = (
        gather_rows(low_proj),
        gather_rows(low_up),
        gather_rows(low_down),
    )
    vec_full = full_vec.astype(jnp.float32)
    gain_one = vec_full[:, 0]
    shift_one = vec_full[:, 1]
    q_bias = vec_full[:, 2]
    v_bias = vec_full[:, 3]
    out_bias = vec_full[:, 4]
    gain_two = vec_full[:, 5]
    shift_two = vec_full[:, 6]
    down_bias = vec_full[:, 7]
    up_bias = vec_full[:, 8:12].T.reshape(FF)
    row_count = tokens.shape[0]
    pack_count = row_count // PACK
    inputs = tokens.astype(jnp.float32)
    normed_one = layer_norm(inputs, gain_one, shift_one).astype(jnp.bfloat16)
    qkv_bias = jnp.concatenate([q_bias, jnp.zeros_like(q_bias), v_bias])
    qkv = (jnp.dot(normed_one, full_attn, preferred_element_type=jnp.float32) + qkv_bias).astype(
        jnp.bfloat16
    )
    qkv_packs = qkv.reshape(pack_count, PACK, 3 * D)
    mixed_rows, log_total = lax.map(attend, (qkv_packs, segment_ids))
    mixed_rows = mixed_rows.reshape(row_count, D)
    residual = (
        inputs + jnp.dot(mixed_rows, full_proj, preferred_element_type=jnp.float32) + out_bias
    )
    normed_two = layer_norm(residual, gain_two, shift_two).astype(jnp.bfloat16)
    pre_act = jnp.dot(normed_two, full_up, preferred_element_type=jnp.float32) + up_bias
    activated = jax.nn.gelu(pre_act).astype(jnp.bfloat16)
    output = (
        residual + jnp.dot(activated, full_down, preferred_element_type=jnp.float32) + down_bias
    )
    grad_rows = cotangent.astype(jnp.float32)
    grad_down = contract_rows(activated, cotangent)
    grad_down_bias = jnp.sum(grad_rows, axis=0)
    grad_act = contract_cols(cotangent, full_down)
    gelu_value, gelu_pull = jax.vjp(jax.nn.gelu, pre_act)
    grad_pre = gelu_pull(grad_act)[0].astype(jnp.bfloat16)
    grad_up = contract_rows(normed_two, grad_pre)
    grad_up_bias = jnp.sum(grad_pre.astype(jnp.float32), axis=0)
    grad_normed_two = contract_cols(grad_pre, full_up)
    norm_value, second_pull = jax.vjp(layer_norm, residual, gain_two, shift_two)
    grad_resid_part, grad_gain_two, grad_shift_two = second_pull(grad_normed_two)
    grad_resid = grad_rows + grad_resid_part
    total_down = reduce_rows(grad_down, "y")
    total_up = reduce_rows(grad_up, "x")
    grad_branch = grad_resid.astype(jnp.bfloat16)
    grad_proj = contract_rows(mixed_rows, grad_branch)
    grad_out_bias = jnp.sum(grad_branch.astype(jnp.float32), axis=0)
    total_proj = reduce_rows(grad_proj, "y")
    grad_mixed = contract_cols(grad_branch, full_proj).astype(jnp.bfloat16)
    grad_qkv = lax.map(
        attend_back, (qkv_packs, segment_ids, log_total, grad_mixed.reshape(pack_count, PACK, D))
    )
    grad_qkv = grad_qkv.reshape(row_count, 3 * D)
    grad_attn = contract_rows(normed_one, grad_qkv)
    qkv_bias_grad = jnp.sum(grad_qkv.astype(jnp.float32), axis=0)
    grad_normed_one = contract_cols(grad_qkv, full_attn)
    first_value, first_pull = jax.vjp(layer_norm, inputs, gain_one, shift_one)
    grad_in_part, grad_gain_one, grad_shift_one = first_pull(grad_normed_one)
    grad_inputs = grad_resid + grad_in_part
    grad_columns = jnp.stack(
        [
            grad_gain_one,
            grad_shift_one,
            qkv_bias_grad[:D],
            qkv_bias_grad[2 * D :],
            grad_out_bias,
            grad_gain_two,
            grad_shift_two,
            grad_down_bias,
        ],
        axis=1,
    )
    grad_vec = jnp.concatenate([grad_columns, grad_up_bias.reshape(4, D).T], axis=1)
    last_block = jnp.concatenate(
        [grad_attn, jnp.pad(grad_vec, ((0, 0), (0, 128 - grad_vec.shape[1])))], axis=1
    )
    total_last = reduce_rows(last_block, "x")
    total_attn, total_vec = total_last[:, : 3 * D], total_last[:, 3 * D : 3 * D + 12]
    attn_upd = adam_step(w_attn, moment_attn, square_attn, total_attn, rate_matrix, weight_decay)
    proj_upd = adam_step(w_proj, moment_proj, square_proj, total_proj, rate_matrix, weight_decay)
    up_upd = adam_step(w_up, moment_up, square_up, total_up, rate_matrix, weight_decay)
    down_upd = adam_step(w_down, moment_down, square_down, total_down, rate_matrix, weight_decay)
    vec_upd = adam_step(vectors, moment_vec, square_vec, total_vec, rate_vector, 0.0)
    return (
        output.astype(jnp.bfloat16),
        grad_inputs,
        attn_upd[0],
        attn_upd[1],
        attn_upd[2],
        proj_upd[0],
        proj_upd[1],
        proj_upd[2],
        up_upd[0],
        up_upd[1],
        up_upd[2],
        down_upd[0],
        down_upd[1],
        down_upd[2],
        vec_upd[0],
        vec_upd[1],
        vec_upd[2],
    )


def solution(mesh):
    in_specs = (
        P(("dp", "fsdp"), None),
        P(("dp", "fsdp"), None),
        P(("dp", "fsdp"), None),
        P("fsdp", None),
        P("fsdp", None),
        P("fsdp", None),
        P("fsdp", None),
        P("fsdp", None),
        P("fsdp", None),
        P("fsdp", None),
        P("fsdp", None),
        P("fsdp", None),
        P("fsdp", None),
        P("fsdp", None),
        P("fsdp", None),
        P("fsdp", None),
        P("fsdp", None),
        P("fsdp", None),
    )
    out_specs = (
        P(("dp", "fsdp"), None),
        P(("dp", "fsdp"), None),
        P("fsdp", None),
        P("fsdp", None),
        P("fsdp", None),
        P("fsdp", None),
        P("fsdp", None),
        P("fsdp", None),
        P("fsdp", None),
        P("fsdp", None),
        P("fsdp", None),
        P("fsdp", None),
        P("fsdp", None),
        P("fsdp", None),
        P("fsdp", None),
        P("fsdp", None),
        P("fsdp", None),
    )
    return jax.shard_map(
        functools.partial(body, *make_comm(mesh)), mesh=mesh, in_specs=in_specs, out_specs=out_specs, check_vma=False)
```

```python
import functools

import jax
import jax.numpy as jnp
from jax import lax
from jax.experimental import pallas as pl
from jax.experimental.pallas import tpu as pltpu
from jax.sharding import PartitionSpec as P

D = 768
HEADS = 12
HEAD = 64
FF = 3072
PACK = 512
STEP = 5
TILE = 64
SPAN = 128


eps_norm = 1e-06
beta_one = 0.5
beta_two = 0.5
rate_matrix = 0.03
rate_vector = 0.25
weight_decay = 0.1
eps_adam = 1e-08
masked_score = -1e30


def layer_norm(rows_in, gain_vec, shift_vec):
    row_mean = jnp.mean(rows_in, axis=-1, keepdims=True)
    centered = rows_in - row_mean
    row_var = jnp.mean(centered * centered, axis=-1, keepdims=True)
    return centered * lax.rsqrt(row_var + eps_norm) * gain_vec + shift_vec


def contract_rows(left, right):
    return lax.dot_general(
        left, right, (((0,), (0,)), ((), ())), preferred_element_type=jnp.float32
    )


def contract_cols(left, right):
    return lax.dot_general(
        left, right, (((1,), (1,)), ((), ())), preferred_element_type=jnp.float32
    )


def stacked(block, low_lanes):
    zero = jnp.zeros_like(block)
    return jnp.concatenate(
        [jnp.where(low_lanes, block, zero), jnp.where(low_lanes, zero, block)], axis=0
    )


def spread(block, low_lanes):
    return jnp.where(low_lanes, block[:TILE], block[TILE:])


def mul_nt(left, right):
    return lax.dot_general(left, right, (((1,), (1,)), ((), ())), preferred_element_type=jnp.float32)


def mul_nn(left, right):
    return lax.dot_general(left, right, (((1,), (0,)), ((), ())), preferred_element_type=jnp.float32)


def mul_tn(left, right):
    return lax.dot_general(left, right, (((0,), (0,)), ((), ())), preferred_element_type=jnp.float32)


def tile_place(tile):
    rows_at = pl.multiple_of(tile * TILE, TILE)
    keys_at = pl.multiple_of(jnp.clip(tile * TILE - 32, 0, PACK - SPAN), 32)
    return pl.ds(rows_at, TILE), pl.ds(keys_at, SPAN)


def soft_rows(queries, key_blocks, same):
    scores = jnp.concatenate([mul_nt(*both) for both in zip(queries, key_blocks)], axis=0)
    scores = jnp.where(same, scores * HEAD ** (-0.5), masked_score)
    exp_scores = jnp.exp(scores - jnp.max(scores, axis=-1, keepdims=True))
    return exp_scores * (1.0 / jnp.sum(exp_scores, axis=-1, keepdims=True))


def same_caption(row_ref, key_ref, rows, tile):
    row_ids = row_ref[rows, :]
    return jnp.concatenate([row_ids] * HEADS, axis=0) == key_ref[0, pl.ds(tile, 1), :]


def parts_of(array):
    return [array[at : at + 2 * TILE] for at in range(0, HEADS * TILE, 2 * TILE)]


def columns(ref, rows, base):
    return [ref[rows, base + at : base + at + 128] for at in range(0, D, 128)]


def attend_kernel(qkv_ref, row_ref, key_ref, out_ref):
    low_lanes = lax.broadcasted_iota(jnp.int32, (TILE, 128), 1) < HEAD

    def step(tile, carry):
        rows, keys = tile_place(tile)
        queries = [stacked(block, low_lanes) for block in columns(qkv_ref, rows, 0)]
        soft = soft_rows(
            queries, columns(qkv_ref, keys, D), same_caption(row_ref, key_ref, rows, tile)
        ).astype(jnp.bfloat16)
        values = columns(qkv_ref, keys, 2 * D)
        mixed = [spread(mul_nn(*both), low_lanes) for both in zip(parts_of(soft), values)]
        out_ref[rows, :] = jnp.concatenate(mixed, axis=1).astype(jnp.bfloat16)
        return carry

    lax.fori_loop(0, PACK // TILE, step, 0)


def attend_back_kernel(qkv_ref, grad_ref, row_ref, key_ref, out_ref, sum_ref, gk_ref, gv_ref):
    low_lanes = lax.broadcasted_iota(jnp.int32, (TILE, 128), 1) < HEAD
    gk_ref[...] = jnp.zeros_like(gk_ref)
    gv_ref[...] = jnp.zeros_like(gv_ref)

    def step(tile, carry):
        rows, keys = tile_place(tile)
        queries = [stacked(block, low_lanes) for block in columns(qkv_ref, rows, 0)]
        grads = [stacked(block, low_lanes) for block in columns(grad_ref, rows, 0)]
        key_blocks = columns(qkv_ref, keys, D)
        values = columns(qkv_ref, keys, 2 * D)
        grad_soft = jnp.concatenate([mul_nt(*both) for both in zip(grads, values)], axis=0)
        soft = soft_rows(queries, key_blocks, same_caption(row_ref, key_ref, rows, tile))
        delta = jnp.sum(soft * grad_soft, axis=-1, keepdims=True)
        grad_score = (soft * (grad_soft - delta)).astype(jnp.bfloat16)
        soft = soft.astype(jnp.bfloat16)
        score_parts = parts_of(grad_score)
        grad_query = [spread(mul_nn(*both), low_lanes) for both in zip(score_parts, key_blocks)]
        grad_query = jnp.concatenate(grad_query, axis=1) * HEAD ** (-0.5)
        out_ref[rows, :D] = grad_query.astype(jnp.bfloat16)
        gk_ref[keys, :] += jnp.concatenate([mul_tn(*both) for both in zip(score_parts, queries)], axis=1)
        gv_ref[keys, :] += jnp.concatenate([mul_tn(*both) for both in zip(parts_of(soft), grads)], axis=1)
        return carry

    lax.fori_loop(0, PACK // TILE, step, 0)
    out_ref[:, D : 2 * D] = (gk_ref[...] * HEAD ** (-0.5)).astype(jnp.bfloat16)
    out_ref[:, 2 * D :] = gv_ref[...].astype(jnp.bfloat16)
    sum_ref[0] = jnp.sum(out_ref[...].astype(jnp.float32), axis=0, keepdims=True)


def pack_rows(cols):
    return pl.BlockSpec((PACK, cols), lambda pack: (pack, 0))


def pack_extra(rows, cols):
    return pl.BlockSpec((1, rows, cols), lambda pack: (pack, 0, 0))


def segment_views(segment_ids):
    starts = [min(max(tile * TILE - 32, 0), PACK - SPAN) for tile in range(PACK // TILE)]
    keys = jnp.stack([segment_ids[:, at : at + SPAN] for at in starts], axis=1)
    return segment_ids.reshape(-1, 1), keys


def attend(qkv, row_ids, key_ids):
    rows = qkv.shape[0]
    return pl.pallas_call(
        attend_kernel,
        grid=(rows // PACK,),
        in_specs=[pack_rows(3 * D), pack_rows(1), pack_extra(PACK // TILE, SPAN)],
        out_specs=pack_rows(D),
        out_shape=jax.ShapeDtypeStruct((rows, D), jnp.bfloat16),
        cost_estimate=pl.CostEstimate(flops=rows * D * 3000, bytes_accessed=rows * D * 8, transcendentals=rows * 12 * 128),
        name="attend",
    )(qkv, row_ids, key_ids)


def attend_back(qkv, grad, row_ids, key_ids):
    rows = qkv.shape[0]
    return pl.pallas_call(
        attend_back_kernel,
        grid=(rows // PACK,),
        in_specs=[pack_rows(3 * D), pack_rows(D), pack_rows(1), pack_extra(PACK // TILE, SPAN)],
        out_specs=[pack_rows(3 * D), pack_extra(1, 3 * D)],
        out_shape=[
            jax.ShapeDtypeStruct((rows, 3 * D), jnp.bfloat16),
            jax.ShapeDtypeStruct((rows // PACK, 1, 3 * D), jnp.float32),
        ],
        scratch_shapes=[pltpu.VMEM((PACK, D), jnp.float32), pltpu.VMEM((PACK, D), jnp.float32)],
        cost_estimate=pl.CostEstimate(flops=rows * D * 9000, bytes_accessed=rows * D * 14, transcendentals=rows * 12 * 128),
        name="attend_back",
    )(qkv, grad, row_ids, key_ids)


ALL_AXES = ("dp", "fsdp")


def take(array, index, axis):
    return lax.dynamic_index_in_dim(array, index, axis, keepdims=False)


def make_comm(mesh):
    dp_size, fsdp_size = mesh.shape["dp"], mesh.shape["fsdp"]

    def gather_plain(shard):
        rows, cols = shard.shape
        piece = rows // dp_size
        mine = lax.dynamic_slice_in_dim(shard, lax.axis_index("dp") * piece, piece, 0)
        full = lax.all_gather(mine, ALL_AXES, axis=0, tiled=True)
        full = full.reshape(dp_size, fsdp_size, piece, cols)
        return full.transpose(1, 0, 2, 3).reshape(fsdp_size * rows, cols)

    def reduce_plain(grad):
        part = lax.psum_scatter(grad.astype(jnp.float32), "fsdp", scatter_dimension=0, tiled=True)
        return lax.psum(part, "dp")

    def place(dev):
        return dev // 16, dev // 8 % 2, dev // 2 % 4, dev % 2

    def index(y, c, z, x):
        return y * 16 + c * 8 + z * 2 + x

    def swap(array, move):
        pairs = [(dev, index(*move(*place(dev)))) for dev in range(32)]
        return lax.ppermute(array, ALL_AXES, pairs)

    def swap_c(array):
        return swap(array, lambda y, c, z, x: (y, 1 - c, z, x))

    def swap_y(array):
        return swap(array, lambda y, c, z, x: (1 - y, c, z, x))

    def swap_xy(array):
        return swap(array, lambda y, c, z, x: (y, c, z, 1 - x) if c == 0 else (1 - y, c, z, x))

    def swap_yx(array):
        return swap(array, lambda y, c, z, x: (1 - y, c, z, x) if c == 0 else (y, c, z, 1 - x))

    def turn_z(array, step):
        return swap(array, lambda y, c, z, x: (y, c, (z + step) % 4, x))

    def spot():
        dp_at, fsdp_at = lax.axis_index("dp"), lax.axis_index("fsdp")
        return dp_at // 2, dp_at % 2, fsdp_at // 2, fsdp_at % 2

    def ordered(bit, mine, other, axis):
        return jnp.stack(
            [jnp.where(bit == 0, mine, other), jnp.where(bit == 0, other, mine)], axis=axis
        )

    def gather_tree(shard):
        y_at, c_at, z_at, x_at = spot()
        rows, cols = shard.shape[0] // 4, shard.shape[1]
        mine = lax.dynamic_slice_in_dim(shard, (y_at * 2 + c_at) * rows, rows, 0)
        around = [mine] + [turn_z(mine, step) for step in (3, 2, 1)]
        lines = lax.dynamic_slice_in_dim(jnp.stack(around + around), 4 - z_at, 4, 0)
        first, second = jnp.where(c_at == 0, x_at, y_at), jnp.where(c_at == 0, y_at, x_at)
        plane = ordered(first, lines, swap_xy(lines), 1)
        cube = ordered(second, plane, swap_yx(plane), 2)
        other = swap_c(cube)
        core_zero = jnp.where(c_at == 0, cube, other)
        core_one = jnp.where(c_at == 0, other, cube)
        full = jnp.stack([core_zero, core_one.swapaxes(1, 2)], axis=3)
        return full.reshape(32 * rows, cols)

    def reduce_tree(grad):
        y_at, c_at, z_at, x_at = spot()
        rows, cols = grad.shape[0] // 32, grad.shape[1]
        low = grad.reshape(4, 2, 2, 2, rows, cols)

        def add(kept, came):
            return (kept.astype(jnp.float32) + came.astype(jnp.float32)).astype(jnp.bfloat16)

        part = add(take(low, c_at, 3), swap_c(take(low, 1 - c_at, 3)))

        def side(flip):
            of_zero = take(part, jnp.bitwise_xor(y_at, flip), 2)
            return jnp.where(c_at == 0, of_zero, take(part, jnp.bitwise_xor(x_at, flip), 1))

        part = add(side(0), swap_yx(side(1)))
        second = jnp.where(c_at == 0, x_at, y_at)
        part = add(take(part, second, 1), swap_xy(take(part, 1 - second, 1)))
        total = take(part, z_at, 0).astype(jnp.float32)
        for step in (2, 1, 3):
            total += turn_z(take(part, (z_at + step) % 4, 0), step).astype(jnp.float32)
        total = total.astype(jnp.bfloat16)
        pair = ordered(y_at, total, swap_y(total), 0)
        quad = ordered(c_at, pair, swap_c(pair), 1)
        return quad.reshape(4 * rows, cols).astype(jnp.float32)

    tree = dp_size == 4 and fsdp_size == 8
    return (gather_tree, reduce_tree) if tree else (gather_plain, reduce_plain)


def adam_step(master, moment, square, gradient, rate, decay_rate):
    moment_new = beta_one * moment + (1.0 - beta_one) * gradient
    square_new = beta_two * square + (1.0 - beta_two) * gradient * gradient
    moment_hat = moment_new / (1.0 - beta_one**STEP)
    square_hat = square_new / (1.0 - beta_two**STEP)
    master_new = master - rate * (
        moment_hat / (jnp.sqrt(square_hat) + eps_adam) + decay_rate * master
    )
    return (master_new, moment_new, square_new)


def body(
    gather_rows,
    reduce_rows,
    tokens,
    cotangent,
    segment_ids,
    w_attn,
    moment_attn,
    square_attn,
    w_proj,
    moment_proj,
    square_proj,
    w_up,
    moment_up,
    square_up,
    w_down,
    moment_down,
    square_down,
    vectors,
    moment_vec,
    square_vec,
):
    low_attn = w_attn.astype(jnp.bfloat16)
    low_proj = w_proj.astype(jnp.bfloat16)
    low_up = w_up.astype(jnp.bfloat16)
    low_down = w_down.astype(jnp.bfloat16)
    low_vec = vectors.astype(jnp.bfloat16)
    first_block = jnp.concatenate(
        [low_attn, jnp.pad(low_vec, ((0, 0), (0, 128 - low_vec.shape[1])))], axis=1
    )
    full_first = gather_rows(first_block)
    full_attn, full_vec = full_first[:, : 3 * D], full_first[:, 3 * D : 3 * D + 12]
    full_second = gather_rows(jnp.concatenate([low_proj, low_up], axis=1))
    full_proj, full_up = full_second[:, :D], full_second[:, D:]
    full_down = gather_rows(low_down)
    vec_full = full_vec.astype(jnp.float32)
    gain_one = vec_full[:, 0]
    shift_one = vec_full[:, 1]
    q_bias = vec_full[:, 2]
    v_bias = vec_full[:, 3]
    out_bias = vec_full[:, 4]
    gain_two = vec_full[:, 5]
    shift_two = vec_full[:, 6]
    down_bias = vec_full[:, 7]
    up_bias = vec_full[:, 8:12].T.reshape(FF)
    inputs = tokens.astype(jnp.float32)
    normed_one = layer_norm(inputs, gain_one, shift_one).astype(jnp.bfloat16)
    qkv_bias = jnp.concatenate([q_bias, jnp.zeros_like(q_bias), v_bias])
    qkv = (jnp.dot(normed_one, full_attn, preferred_element_type=jnp.float32) + qkv_bias).astype(
        jnp.bfloat16
    )
    row_ids, key_ids = segment_views(segment_ids)
    mixed_rows = attend(qkv, row_ids, key_ids)
    residual = (
        inputs + jnp.dot(mixed_rows, full_proj, preferred_element_type=jnp.float32) + out_bias
    )
    normed_two = layer_norm(residual, gain_two, shift_two).astype(jnp.bfloat16)
    pre_act = jnp.dot(normed_two, full_up, preferred_element_type=jnp.float32) + up_bias
    activated = jax.nn.gelu(pre_act).astype(jnp.bfloat16)
    output = (
        residual + jnp.dot(activated, full_down, preferred_element_type=jnp.float32) + down_bias
    )
    grad_rows = cotangent.astype(jnp.float32)
    grad_down = contract_rows(activated, cotangent).astype(jnp.bfloat16)
    total_down = reduce_rows(grad_down)
    grad_down_bias = jnp.sum(grad_rows, axis=0)
    grad_act = contract_cols(cotangent, full_down)
    gelu_value, gelu_pull = jax.vjp(jax.nn.gelu, pre_act)
    grad_pre = gelu_pull(grad_act)[0].astype(jnp.bfloat16)
    grad_up = contract_rows(normed_two, grad_pre).astype(jnp.bfloat16)
    grad_up_bias = jnp.sum(grad_pre.astype(jnp.float32), axis=0)
    grad_normed_two = contract_cols(grad_pre, full_up)
    norm_value, second_pull = jax.vjp(layer_norm, residual, gain_two, shift_two)
    grad_resid_part, grad_gain_two, grad_shift_two = second_pull(grad_normed_two)
    grad_resid = grad_rows + grad_resid_part
    grad_branch = grad_resid.astype(jnp.bfloat16)
    grad_proj = contract_rows(mixed_rows, grad_branch).astype(jnp.bfloat16)
    total_second = reduce_rows(jnp.concatenate([grad_proj, grad_up], axis=1))
    total_proj, total_up = total_second[:, :D], total_second[:, D:]
    grad_out_bias = jnp.sum(grad_branch.astype(jnp.float32), axis=0)
    grad_mixed = contract_cols(grad_branch, full_proj).astype(jnp.bfloat16)
    grad_qkv, qkv_sums = attend_back(qkv, grad_mixed, row_ids, key_ids)
    grad_attn = contract_rows(normed_one, grad_qkv).astype(jnp.bfloat16)
    qkv_bias_grad = jnp.sum(qkv_sums, axis=(0, 1))
    grad_normed_one = contract_cols(grad_qkv, full_attn)
    first_value, first_pull = jax.vjp(layer_norm, inputs, gain_one, shift_one)
    grad_in_part, grad_gain_one, grad_shift_one = first_pull(grad_normed_one)
    grad_inputs = grad_resid + grad_in_part
    grad_columns = jnp.stack(
        [
            grad_gain_one,
            grad_shift_one,
            qkv_bias_grad[:D],
            qkv_bias_grad[2 * D :],
            grad_out_bias,
            grad_gain_two,
            grad_shift_two,
            grad_down_bias,
        ],
        axis=1,
    )
    grad_vec = jnp.concatenate([grad_columns, grad_up_bias.reshape(4, D).T], axis=1)
    last_block = jnp.concatenate(
        [grad_attn, jnp.pad(grad_vec, ((0, 0), (0, 128 - grad_vec.shape[1]))).astype(jnp.bfloat16)], axis=1
    )
    total_last = reduce_rows(last_block)
    total_attn, total_vec = total_last[:, : 3 * D], total_last[:, 3 * D : 3 * D + 12]
    attn_upd = adam_step(w_attn, moment_attn, square_attn, total_attn, rate_matrix, weight_decay)
    proj_upd = adam_step(w_proj, moment_proj, square_proj, total_proj, rate_matrix, weight_decay)
    up_upd = adam_step(w_up, moment_up, square_up, total_up, rate_matrix, weight_decay)
    down_upd = adam_step(w_down, moment_down, square_down, total_down, rate_matrix, weight_decay)
    vec_upd = adam_step(vectors, moment_vec, square_vec, total_vec, rate_vector, 0.0)
    return (
        output.astype(jnp.bfloat16),
        grad_inputs,
        attn_upd[0],
        attn_upd[1],
        attn_upd[2],
        proj_upd[0],
        proj_upd[1],
        proj_upd[2],
        up_upd[0],
        up_upd[1],
        up_upd[2],
        down_upd[0],
        down_upd[1],
        down_upd[2],
        vec_upd[0],
        vec_upd[1],
        vec_upd[2],
    )


def solution(mesh):
    in_specs = (
        P(("dp", "fsdp"), None),
        P(("dp", "fsdp"), None),
        P(("dp", "fsdp"), None),
        P("fsdp", None),
        P("fsdp", None),
        P("fsdp", None),
        P("fsdp", None),
        P("fsdp", None),
        P("fsdp", None),
        P("fsdp", None),
        P("fsdp", None),
        P("fsdp", None),
        P("fsdp", None),
        P("fsdp", None),
        P("fsdp", None),
        P("fsdp", None),
        P("fsdp", None),
        P("fsdp", None),
    )
    out_specs = (
        P(("dp", "fsdp"), None),
        P(("dp", "fsdp"), None),
        P("fsdp", None),
        P("fsdp", None),
        P("fsdp", None),
        P("fsdp", None),
        P("fsdp", None),
        P("fsdp", None),
        P("fsdp", None),
        P("fsdp", None),
        P("fsdp", None),
        P("fsdp", None),
        P("fsdp", None),
        P("fsdp", None),
        P("fsdp", None),
        P("fsdp", None),
        P("fsdp", None),
    )
    return jax.shard_map(
        functools.partial(body, *make_comm(mesh)), mesh=mesh, in_specs=in_specs, out_specs=out_specs, check_vma=False)
```
